256 devices in a mesh: bead: 16 (over x, y_hi, core), atom: 16 (over y_lo, z).
Axes of the slice: x: 4, y: 4 (y_hi: 2, y_lo: 2; y = y_hi * 2 + y_lo), z: 8, core: 2. Of those that a mesh axis runs over, the one named last changes fastest.
Arguments:
- positions: float32 [3, 16, 4096], P(None, 'bead', 'atom'), may hold values from -1 to 35, as said below
- velocities: float32 [3, 16, 4096], P(None, 'bead', 'atom'), may hold values from -3 to 3
- forces_now: float32 [3, 16, 4096], P(None, 'bead', 'atom'), may hold values from -18 to 18
- masses: float32 [4096], P('atom'), may hold values from 1 to 16
- features: bfloat16 [16, 256, 4096], P('bead', None, 'atom'), may hold values from -6 to 6
- tile_blocks: int32 [32, 9], P('atom'), may hold values from 0 to 31, as said below
- block_slots: int32 [4096], P('atom'), may hold values from 0 to 4095, as said below
- w_basis: bfloat16 [64, 32], replicated, may hold values from -1 to 1
- w_feat: bfloat16 [64, 256], replicated, may hold values from -0.375 to 0.375
- hidden_bias: float32 [64], replicated, may hold values from -5 to 5
- w_out: float32 [64], replicated, may hold values from -0.03 to 0.03
Outputs:
- positions_next: float32 [3, 16, 4096], P(None, 'bead', 'atom')
- velocities_next: float32 [3, 16, 4096], P(None, 'bead', 'atom')
- forces_next: float32 [3, 16, 4096], P(None, 'bead', 'atom')
The draws below stay inside these ranges and needn't reach their ends.
Inputs may be any that keep to these rules, and one draw needn't show every extreme that they name: `tile_blocks`: every entry of row k is one of the blocks k - 4 to k + 4, counted cyclically over the 32 blocks; blocks k - 4 and k + 4 are always named; the other entries may repeat; the order is drawn for each row. `block_slots`: the entries j * 256 to (j + 1) * 256 - 1 are a permutation of the atom numbers j * 256 to (j + 1) * 256 - 1. `positions`: the beads of one atom lie within 0.06, in each coordinate, of a common centre whose first two coordinates lie in [0, 2.9) and whose third lies in [0.15 k, 0.15 (k + 1)), k the block of the atom's slot.
All inputs are finite; a program needn't handle non-finite values.
Results may differ from the reference program's by a relative error of at most 0.0003.
Values may be sent and summed in bfloat16 or wider, within the bound.
No kernel may reach another device: no remote copies, remote signals or barrier semaphores. Data moves between devices by JAX's collectives and lax.ppermute only.
A program may use at most 128 MiB of HBM per device.

```python
import math
import jax
import jax.numpy as jnp
from jax import lax

TILE = 128
NB = 32
HID = 64
FEAT = 256
TPB = 9
BLK_DEV = 2
ATOM_DEV = 256
BLOCKS = 32
ATOMS = 4096
BEADS = 16


def slot_layout(key):
    stretches = ATOMS // ATOM_DEV
    scores = jax.random.randint(key, (stretches, ATOM_DEV), 0, 1 << 16) * ATOM_DEV + jnp.arange(ATOM_DEV, dtype=jnp.int32)[None, :]
    return jnp.argsort(scores, axis=1).astype(jnp.int32)


def draw_block_slots(key, part):
    local_order = slot_layout(jax.random.fold_in(key, 11))
    stretch_base = jnp.arange(ATOMS // ATOM_DEV, dtype=jnp.int32)[:, None] * ATOM_DEV
    return (local_order + stretch_base).reshape(ATOMS).astype(jnp.int32)


def draw_positions(key, part):
    local_order = slot_layout(jax.random.fold_in(key, 11))
    slot_of = jnp.argsort(local_order, axis=1).astype(jnp.int32)
    stretch_ids = jnp.arange(ATOMS // ATOM_DEV, dtype=jnp.int32)[:, None]
    block_of = (stretch_ids * BLK_DEV + slot_of // TILE).reshape(ATOMS).astype(jnp.float32)
    key_one, key_two, key_three = jax.random.split(jax.random.fold_in(key, 23), 3)
    plane_xy = jax.random.uniform(key_one, (2, ATOMS), jnp.float32) * 2.9
    height = (block_of + jax.random.uniform(key_two, (ATOMS,), jnp.float32)) * 0.15
    centre_pos = jnp.concatenate([plane_xy, height[None, :]], axis=0)
    bead_noise = jnp.clip(jax.random.normal(key_three, (3, BEADS, ATOMS), jnp.float32) * 0.015, -0.06, 0.06)
    return (centre_pos[:, None, :] + bead_noise).astype(jnp.float32)


def draw_tile_blocks(key, part):
    key_one, key_two = jax.random.split(jax.random.fold_in(key, 37), 2)
    fixed_low = jnp.full((BLOCKS, 1), -4, jnp.int32)
    fixed_high = jnp.full((BLOCKS, 1), 4, jnp.int32)
    drawn = jax.random.randint(key_one, (BLOCKS, TPB - 2), -4, 5).astype(jnp.int32)
    values = jnp.concatenate([fixed_low, fixed_high, drawn], axis=1)
    scores = jax.random.randint(key_two, (BLOCKS, TPB), 0, 1 << 16) * TPB + jnp.arange(TPB, dtype=jnp.int32)[None, :]
    order = jnp.argsort(scores, axis=1).astype(jnp.int32)
    shuffled = jnp.take_along_axis(values, order, axis=1)
    row_ids = jnp.arange(BLOCKS, dtype=jnp.int32)[:, None]
    return ((row_ids + shuffled) % BLOCKS).astype(jnp.int32)


def levels(key, shape, cuts, smallest, largest):
    factor_of, own = 1.0, jax.random.fold_in(key, 6)
    for position, blocks in cuts:
        steps = jnp.exp(jax.random.uniform(jax.random.fold_in(own, position), (blocks,), jnp.float32, smallest / len(cuts), largest / len(cuts)))
        factor_of = factor_of * jnp.repeat(steps, shape[position] // blocks).reshape([-1 if axis == position else 1 for axis in range(len(shape))])
    return factor_of


def noise(own_key, dims, deviation, bound, shards=(), kind=jnp.bfloat16):
    array = jax.random.normal(own_key, dims, jnp.float32) * deviation
    if len(shards) > 0:
        array = levels(own_key, dims, shards, -0.22, 0.18) * array
    return jnp.clip(array, min=-bound, max=bound).astype(kind)


def setup_inputs(seed: int = 0) -> dict:
    seeds = jax.random.split(jax.random.key(seed), 12)
    positions = draw_positions(jax.random.fold_in(seeds[11], 71), 0)
    velocities = noise(seeds[1], (3, BEADS, ATOMS), 0.5, 3.0, ((1, 16), (2, 16)), jnp.float32)
    forces_now = noise(seeds[2], (3, BEADS, ATOMS), 3.0, 18.0, ((1, 16), (2, 16)), jnp.float32)
    masses = jnp.clip(jnp.exp(math.log(16.0) - 2.7725887 * jax.random.uniform(seeds[3], (ATOMS,), jnp.float32) ** levels(seeds[3], (ATOMS,), ((0, 16),), -0.2, 0.2)), 1.0, 16.0)
    features = noise(seeds[4], (BEADS, FEAT, ATOMS), 1.0, 6.0, ((0, 16), (2, 16)))
    tile_blocks = draw_tile_blocks(jax.random.fold_in(seeds[11], 71), 0)
    block_slots = draw_block_slots(jax.random.fold_in(seeds[11], 71), 0)
    w_basis = noise(seeds[7], (HID, NB), NB ** -0.5, 1.0)
    w_feat = noise(seeds[8], (HID, FEAT), FEAT ** -0.5, 0.375)
    hidden_bias = noise(seeds[9], (HID,), 1.0, 5.0, (), jnp.float32)
    w_out = noise(seeds[10], (HID,), 0.005, 0.03, (), jnp.float32)
    return {"positions": positions, "velocities": velocities, "forces_now": forces_now, "masses": masses, "features": features, "tile_blocks": tile_blocks, "block_slots": block_slots, "w_basis": w_basis, "w_feat": w_feat, "hidden_bias": hidden_bias, "w_out": w_out}


LAYER_WIDTH = 0.15
SIDE_LENGTH = 2.9
CUTOFF = 0.6
BASIS_SHARPNESS = 355.0
SOFTEN = 0.0001
TIME_STEP = 0.1
OMEGA_SQ = 100.0
rows_per_turn = 16

def pair_terms(q_rows, p_rows, q_cols, p_cols, self_mask, w_basis, hidden_bias, w_out, box_depth):
    box_size = jnp.stack([jnp.float32(SIDE_LENGTH), jnp.float32(SIDE_LENGTH), jnp.float32(box_depth)]).reshape(3, 1, 1)
    displace = q_cols[:, None, :] - q_rows[:, :, None]
    displace = displace - box_size * jnp.floor(displace / box_size + 0.5)
    dist_sq = lax.optimization_barrier(jnp.sum(displace * displace, axis=0))
    distance = jnp.sqrt(dist_sq + SOFTEN)
    inner_part = jnp.maximum(1.0 - dist_sq / (CUTOFF * CUTOFF), 0.0)
    smooth = inner_part * inner_part
    smooth_slope = -2.0 * inner_part / (CUTOFF * CUTOFF)
    basis_count = w_basis.shape[1]
    centres = (CUTOFF * (jnp.arange(basis_count, dtype=jnp.float32) + 0.5) / basis_count).reshape(basis_count, 1, 1)
    offset = distance[None] - centres
    basis_vals = jnp.exp(-BASIS_SHARPNESS * offset * offset)
    row_count, col_count = dist_sq.shape
    basis_half = basis_vals.astype(jnp.bfloat16).reshape(basis_count, row_count * col_count)
    pre_act = jnp.dot(w_basis, basis_half, preferred_element_type=jnp.float32).reshape(-1, row_count, col_count)
    pre_act = pre_act + p_rows.astype(jnp.float32)[:, :, None] + p_cols.astype(jnp.float32)[:, None, :] + hidden_bias[:, None, None]
    activation = jnp.tanh(pre_act)
    energy = lax.optimization_barrier(jnp.sum(w_out[:, None, None] * activation, axis=0))
    back_grad = (w_out[:, None, None] * (1.0 - activation * activation)).astype(jnp.bfloat16).reshape(-1, row_count * col_count)
    grad_basis = lax.dot_general(w_basis, back_grad, (((0,), (0,)), ((), ())), preferred_element_type=jnp.float32).reshape(basis_count, row_count, col_count)
    dbasis = -BASIS_SHARPNESS * offset * basis_vals / distance[None]
    de_ds = smooth_slope * energy + smooth * lax.optimization_barrier(jnp.sum(grad_basis * dbasis, axis=0))
    de_ds = jnp.where(self_mask, 0.0, de_ds)
    return lax.optimization_barrier(jnp.sum(2.0 * de_ds[None] * displace, axis=2))

def block_forces(pos_all, proj_all, own_block, sources, w_basis, hidden_bias, w_out, box_depth):
    start = (own_block * TILE).astype(jnp.int32)
    pos_own = lax.dynamic_slice_in_dim(pos_all, start, TILE, 1)
    proj_own = lax.dynamic_slice_in_dim(proj_all, start, TILE, 1)
    tile_count = sources.shape[0]
    q_cols = jnp.concatenate([lax.dynamic_slice_in_dim(pos_all, (sources[k] * TILE).astype(jnp.int32), TILE, 1) for k in range(tile_count)], axis=1)
    p_cols = jnp.concatenate([lax.dynamic_slice_in_dim(proj_all, (sources[k] * TILE).astype(jnp.int32), TILE, 1) for k in range(tile_count)], axis=1)
    col_source = jnp.repeat(sources.astype(jnp.int32), TILE)
    col_local = jnp.tile(jnp.arange(TILE, dtype=jnp.int32), tile_count)
    row_ids = jnp.arange(rows_per_turn, dtype=jnp.int32)
    pieces = []
    for group_idx in range(TILE // rows_per_turn):
        low = group_idx * rows_per_turn
        q_rows = pos_own[:, low:low + rows_per_turn]
        p_rows = proj_own[:, low:low + rows_per_turn]
        self_mask = (col_source[None, :] == own_block) & (row_ids[:, None] + low == col_local[None, :])
        pieces.append(pair_terms(q_rows, p_rows, q_cols, p_cols, self_mask, w_basis, hidden_bias, w_out, box_depth))
    return jnp.concatenate(pieces, axis=1)

def reference(positions, velocities, forces_now, masses, features, tile_blocks, block_slots, w_basis, w_feat, hidden_bias, w_out):
    half_vel = velocities + 0.5 * TIME_STEP * forces_now / masses
    moved_pos = positions + TIME_STEP * half_vel
    sorted_pos = moved_pos[:, :, block_slots]
    sorted_feat = features[:, :, block_slots]
    projected = lax.map(lambda feats: jnp.dot(w_feat, feats, preferred_element_type=jnp.float32).astype(jnp.bfloat16), sorted_feat)
    box_depth = BLOCKS * LAYER_WIDTH

    def bead_forces(pair_in):
        pos_bead, proj_bead = pair_in
        per_block = lax.map(lambda block_idx: block_forces(pos_bead, proj_bead, block_idx, tile_blocks[block_idx], w_basis, hidden_bias, w_out, box_depth), jnp.arange(BLOCKS, dtype=jnp.int32))
        return jnp.transpose(per_block, (1, 0, 2)).reshape(3, BLOCKS * TILE)
    pair_sorted = lax.map(bead_forces, (jnp.transpose(sorted_pos, (1, 0, 2)), projected))
    pair_sorted = jnp.transpose(pair_sorted, (1, 0, 2))
    pair_force = jnp.zeros_like(moved_pos).at[:, :, block_slots].set(pair_sorted)
    spring = -OMEGA_SQ * masses * (2.0 * moved_pos - jnp.roll(moved_pos, 1, axis=1) - jnp.roll(moved_pos, -1, axis=1))
    forces_next = pair_force + spring
    velocities_next = half_vel + 0.5 * TIME_STEP * forces_next / masses
    return (moved_pos, velocities_next, forces_next)
```

```python
import functools

import jax
import jax.numpy as jnp
from jax import lax
from jax.experimental import pallas as pl
from jax.experimental.pallas import tpu as pltpu
from jax.sharding import PartitionSpec as P

TILE = 128
NB = 32
HID = 64
LANES = 128
SUB = 8
CAP = 8
GROUPS = LANES // CAP
PAY = 80
HALO = 2
REACH = 4
DELTAS = 2 * REACH + 1

LAYER_WIDTH = 0.15
SIDE_LENGTH = 2.9
CUTOFF = 0.6
BASIS_SHARPNESS = 355.0
SOFTEN = 0.0001
TIME_STEP = 0.1
OMEGA_SQ = 100.0

F32 = jnp.float32
BF16 = jnp.bfloat16
I32 = jnp.int32


def split3(x):
    hi = x.astype(BF16).astype(F32)
    rest = x - hi
    mid = rest.astype(BF16).astype(F32)
    return hi, mid, rest - mid


def dot(a, b):
    return jnp.dot(a, b, preferred_element_type=F32)


def dot_nt(a, b):
    return lax.dot_general(a, b, (((1,), (1,)), ((), ())), preferred_element_type=F32)


def head_kernel(pos, vel, force, mass, feat, slots, w_feat, moved, payload):
    atoms = pos.shape[2]
    m = mass[...]
    parts = [[], [], []]
    for c in range(3):
        half = vel[c] + 0.5 * TIME_STEP * force[c] / m
        new = pos[c] + TIME_STEP * half
        moved[c] = new
        for k, part in enumerate(split3(new)):
            parts[k].append(part)
    rows = parts[0] + parts[1] + parts[2] + [jnp.zeros((PAY - HID - 9, atoms), F32)]
    coords = jnp.concatenate(rows, axis=0).astype(BF16)
    projected = dot(w_feat[...], feat[0]).astype(BF16)
    local = slots[...] & (atoms - 1)
    atom_ids = lax.broadcasted_iota(I32, (atoms, atoms), 0)
    pick = jnp.where(atom_ids == local, 1.0, 0.0).astype(BF16)
    ordered = dot(jnp.concatenate([projected, coords], axis=0), pick).astype(BF16)
    for b in range(atoms // TILE):
        payload[b] = ordered[:, b * TILE : (b + 1) * TILE]


def wrap(c, length):
    return c - length * jnp.floor(c * (1.0 / length) + 0.5)


def pair_kernel(
    blocks_all,
    tiles,
    pos,
    vel,
    force,
    mass,
    slots,
    w_basis,
    w_basis_t,
    bias,
    w_out,
    low2,
    low1,
    own,
    high1,
    high2,
    moved,
    bead_low,
    bead_high,
    vel_next,
    force_next,
    coord_s,
    proj_s,
    list_s,
    lhs_s,
    wout_s,
    acc_s,
    count_s,
    pass_s,
):
    atoms = pos.shape[2]
    here = atoms // TILE
    first = lax.axis_index("atom") * here
    box = (SIDE_LENGTH, SIDE_LENGTH, blocks_all * LAYER_WIDTH)

    for rb in range(here):
        for d in range(DELTAS):
            count_s[rb, d] = 0
        for j in range(DELTAS):
            off = tiles[rb, j] - (first + rb) + REACH
            off = jnp.where(off < 0, off + blocks_all, off)
            off = jnp.where(off >= blocks_all, off - blocks_all, off)
            count_s[rb, off] = count_s[rb, off] + 1

    for src, ref in enumerate((low2, low1, own, high1, high2)):
        for b in range(here):
            block = ref[b].astype(F32)
            proj_s[src * here + b] = block[:HID]
            xyz = block[HID : HID + 3] + block[HID + 3 : HID + 6] + block[HID + 6 : HID + 9]
            coord_s[src * here + b] = jnp.concatenate([xyz, jnp.zeros((5, TILE), F32)], axis=0)

    lane = lax.broadcasted_iota(I32, (SUB, LANES), 1)
    sub = lax.broadcasted_iota(I32, (SUB, LANES), 0)
    group = lane // CAP

    eye = lax.broadcasted_iota(I32, (HID, HID), 0) == lax.broadcasted_iota(I32, (HID, HID), 1)
    bias_col = jnp.sum(jnp.where(eye, bias[...], 0.0), axis=1, keepdims=True)
    wout_col = jnp.sum(jnp.where(eye, w_out[...], 0.0), axis=1, keepdims=True)
    wout_s[...] = jnp.broadcast_to(wout_col, (HID, LANES))
    bias_parts = split3(bias_col)

    col = lax.broadcasted_iota(I32, (HID, HID), 1)
    place = (
        lax.broadcasted_iota(I32, (NB, HID), 0) == lax.broadcasted_iota(I32, (NB, HID), 1)
    )
    base = dot(w_basis[...], jnp.where(place, 1.0, 0.0).astype(BF16))
    for k in range(3):
        base = jnp.where(col == NB + GROUPS + k, bias_parts[k], base)
    row_l = lax.broadcasted_iota(I32, (TILE, HID), 0)
    col_l = lax.broadcasted_iota(I32, (TILE, HID), 1)
    for rb in range(here):
        for r in range(SUB):
            sel = (row_l == SUB * (col_l - NB) + r) & (col_l < NB + GROUPS)
            mine = dot(own[rb, :HID, :], jnp.where(sel, 1.0, 0.0).astype(BF16))
            lhs_s[rb, r] = (base + mine).astype(BF16)

    k_row = lax.broadcasted_iota(I32, (HID - NB, LANES), 0)
    k_grp = lax.broadcasted_iota(I32, (HID - NB, LANES), 1) // CAP
    fixed = jnp.where((k_row == k_grp) | ((k_row >= GROUPS) & (k_row < GROUPS + 3)), 1.0, 0.0)
    fixed = fixed.astype(BF16)

    upper = (
        lax.broadcasted_iota(I32, (LANES, LANES), 0) < lax.broadcasted_iota(I32, (LANES, LANES), 1)
    )
    upper = jnp.where(upper, 1.0, 0.0).astype(BF16)
    lane_t = lax.broadcasted_iota(I32, (TILE, LANES), 1)
    row_t = lax.broadcasted_iota(I32, (TILE, LANES), 0)
    tag = (lane_t * 257 + 65536).astype(F32)
    centre = (lax.broadcasted_iota(I32, (NB, 1), 0).astype(F32) + 0.5) * (CUTOFF / NB)

    forces = []
    for rb in range(here):
        block_own = HALO * here + rb
        cols = jnp.transpose(coord_s[block_own])
        row_xyz = [jnp.broadcast_to(cols[:, c : c + 1], (TILE, LANES)) for c in range(3)]

        def build(d, carry):
            @pl.when(count_s[rb, d] > 0)
            def _():
                block = block_own + d - REACH
                d2 = jnp.zeros((TILE, LANES), F32)
                for c in range(3):
                    diff = wrap(coord_s[block, c : c + 1, :] - row_xyz[c], box[c])
                    d2 = d2 + diff * diff
                self_lane = row_t + jnp.where(d == REACH, 0, 1024)
                near = (d2 < CUTOFF * CUTOFF) & (lane_t != self_lane)
                mask = jnp.where(near, 1.0, 0.0)
                rank = dot(mask.astype(BF16), upper)
                fullest = jnp.max(rank + mask)
                pass_s[d] = (fullest.astype(I32) + (CAP - 1)) // CAP
                v = jnp.where(near, tag - 256.0 * rank, 0.0).astype(I32)
                for bit in range(7):
                    go = jnp.where((v & (256 << bit)) != 0, v, 0)
                    v = (v ^ go) | pltpu.roll(go, LANES - (1 << bit), 1)
                for o in range(GROUPS):
                    piece = v[SUB * o : SUB * (o + 1)]
                    list_s[d, o] = piece if o == 0 else pltpu.roll(piece, CAP * o, 1)

            @pl.when(count_s[rb, d] == 0)
            def _():
                pass_s[d] = 0

            return carry

        lax.fori_loop(0, DELTAS, build, 0)

        mine = []
        for c in range(3):
            m = jnp.zeros((SUB, LANES), F32)
            for o in range(GROUPS):
                m = jnp.where(group == o, row_xyz[c][SUB * o : SUB * (o + 1)], m)
            mine.append(m)
        acc_s[...] = jnp.zeros_like(acc_s)

        def visit(d, carry):
            block = block_own + d - REACH
            times = 2.0 * count_s[rb, d].astype(F32)

            def one_pass(p, inner):
                here_group = (group - p) & (GROUPS - 1)
                level = [list_s[d, o] for o in range(GROUPS)]
                bit = 1
                while len(level) > 1:
                    odd = (here_group & bit) != 0
                    level = [
                        jnp.where(odd, level[2 * i + 1], level[2 * i])
                        for i in range(len(level) // 2)
                    ]
                    bit *= 2
                slot = pltpu.roll(level[0], (LANES - CAP * p) & (LANES - 1), 1)
                idx = slot & (LANES - 1)
                live = slot >= 65536
                diff = []
                d2 = jnp.zeros((SUB, LANES), F32)
                for c in range(3):
                    table = jnp.broadcast_to(coord_s[block, c : c + 1, :], (SUB, LANES))
                    there = jnp.take_along_axis(table, idx, axis=1, mode="promise_in_bounds")
                    one = wrap(there - mine[c], box[c])
                    diff.append(one)
                    d2 = d2 + one * one
                distance = jnp.sqrt(d2 + SOFTEN)
                inner_part = jnp.maximum(1.0 - d2 / (CUTOFF * CUTOFF), 0.0)
                smooth = inner_part * inner_part * (-BASIS_SHARPNESS / distance)
                slope = inner_part * (-2.0 / (CUTOFF * CUTOFF))
                table = proj_s[block]
                w_o = wout_s[...]
                energies = []
                grads = []
                for r in range(SUB):
                    offset = distance[r : r + 1, :] - centre
                    basis = jnp.exp(-BASIS_SHARPNESS * offset * offset)
                    right = jnp.concatenate([basis.astype(BF16), fixed], axis=0)
                    pre = dot(lhs_s[rb, r], right)
                    at = jnp.broadcast_to(idx[r : r + 1, :], (HID, LANES))
                    pre = pre + jnp.take_along_axis(table, at, axis=1, mode="promise_in_bounds")
                    act = jnp.tanh(pre)
                    part = w_o * act
                    energies.append(jnp.sum(part, axis=0, keepdims=True))
                    back = (w_o - part * act).astype(BF16)
                    grad = dot(w_basis_t[...], back)
                    grads.append(jnp.sum(grad * (offset * basis), axis=0, keepdims=True))
                energy = jnp.concatenate(energies, axis=0)
                grad = jnp.concatenate(grads, axis=0)
                coef = jnp.where(live, times * (slope * energy + smooth * grad), 0.0)
                for c in range(3):
                    acc_s[c] = acc_s[c] + coef * diff[c]
                return inner

            return lax.fori_loop(0, pass_s[d], one_pass, carry)

        lax.fori_loop(0, DELTAS, visit, 0)

        rows = []
        for c in range(3):
            a = acc_s[c]
            for step in (1, 2, 4):
                down = pltpu.roll(a, LANES - step, 1)
                up = pltpu.roll(a, step, 1)
                a = a + jnp.where((lane & step) == 0, down, up)
            a = jnp.where((lane & (CAP - 1)) == sub, a, 0.0)
            rows.append(jnp.sum(a, axis=0, keepdims=True))
        forces.append(rows)

    full = [jnp.concatenate([forces[rb][c] for rb in range(here)], axis=1) for c in range(3)]
    parts = [split3(f) for f in full]
    stacked = [parts[c][k] for k in range(3) for c in range(3)]
    stacked = jnp.concatenate(stacked + [jnp.zeros((7, atoms), F32)], axis=0).astype(BF16)
    local = slots[...] & (atoms - 1)
    atom_ids = lax.broadcasted_iota(I32, (atoms, atoms), 0)
    pick = jnp.where(atom_ids == local, 1.0, 0.0).astype(BF16)
    placed = dot_nt(stacked, pick)
    m = mass[...]
    for c in range(3):
        pair = placed[c : c + 1] + placed[3 + c : 4 + c] + placed[6 + c : 7 + c]
        half = vel[c] + 0.5 * TIME_STEP * force[c] / m
        spring = -OMEGA_SQ * m * (2.0 * moved[c] - bead_low[c] - bead_high[c])
        total = pair + spring
        force_next[c] = total
        vel_next[c] = half + 0.5 * TIME_STEP * total / m


def shifted(block, axis, distance):
    count = lax.axis_size(axis)
    return lax.ppermute(block, axis, [((i - distance) % count, i) for i in range(count)])


def body(
    positions,
    velocities,
    forces_now,
    masses,
    features,
    tile_blocks,
    block_slots,
    w_basis,
    w_feat,
    hidden_bias,
    w_out,
):
    atoms = positions.shape[2]
    here = atoms // TILE
    blocks_all = here * lax.axis_size("atom")
    mass = masses.reshape(1, atoms)
    slots = block_slots.reshape(1, atoms)
    moved, payload = pl.pallas_call(
        head_kernel,
        out_shape=(
            jax.ShapeDtypeStruct(positions.shape, F32),
            jax.ShapeDtypeStruct((here, PAY, TILE), BF16),
        ),
        name="head",
    )(positions, velocities, forces_now, mass, features, slots, w_feat)
    near = [shifted(payload, "atom", s) for s in (2, 1, -1, -2)]
    bead_low = shifted(moved, "bead", 1)
    bead_high = shifted(moved, "bead", -1)
    vmem = pl.BlockSpec(memory_space=pltpu.VMEM)
    sources = 2 * HALO + 1
    vel_next, force_next = pl.pallas_call(
        functools.partial(pair_kernel, blocks_all),
        out_shape=(
            jax.ShapeDtypeStruct(positions.shape, F32),
            jax.ShapeDtypeStruct(positions.shape, F32),
        ),
        in_specs=[pl.BlockSpec(memory_space=pltpu.SMEM)] + [vmem] * 17,
        out_specs=(vmem, vmem),
        scratch_shapes=[
            pltpu.VMEM((sources * here, SUB, TILE), F32),
            pltpu.VMEM((sources * here, HID, TILE), F32),
            pltpu.VMEM((DELTAS, GROUPS, SUB, LANES), I32),
            pltpu.VMEM((here, SUB, HID, HID), BF16),
            pltpu.VMEM((HID, LANES), F32),
            pltpu.VMEM((3, SUB, LANES), F32),
            pltpu.SMEM((here, DELTAS), I32),
            pltpu.SMEM((DELTAS,), I32),
        ],
        name="pairs",
    )(
        tile_blocks,
        positions,
        velocities,
        forces_now,
        mass,
        slots,
        w_basis,
        w_basis.T,
        hidden_bias.reshape(1, HID),
        w_out.reshape(1, HID),
        near[0],
        near[1],
        payload,
        near[2],
        near[3],
        moved,
        bead_low,
        bead_high,
    )
    return (moved, vel_next, force_next)


def solution(mesh):
    return jax.shard_map(
        body,
        mesh=mesh,
        in_specs=(
            P(None, "bead", "atom"),
            P(None, "bead", "atom"),
            P(None, "bead", "atom"),
            P("atom"),
            P("bead", None, "atom"),
            P("atom", None),
            P("atom"),
            P(),
            P(),
            P(),
            P(),
        ),
        out_specs=(P(None, "bead", "atom"), P(None, "bead", "atom"), P(None, "bead", "atom")),
        check_vma=False,
    )
```

```python
import functools

import jax
import jax.numpy as jnp
from jax import lax
from jax.experimental import pallas as pl
from jax.experimental.pallas import tpu as pltpu
from jax.sharding import PartitionSpec as P

TILE = 128
NB = 32
HID = 64
LANES = 128
SUB = 8
CAP = 8
GROUPS = LANES // CAP
PAY = 80
UNROLL = 3
BUILD = 2
HALO = 2
REACH = 4
DELTAS = 2 * REACH + 1

LAYER_WIDTH = 0.15
SIDE_LENGTH = 2.9
CUTOFF = 0.6
BASIS_SHARPNESS = 355.0
SOFTEN = 0.0001
TIME_STEP = 0.1
OMEGA_SQ = 100.0

F32 = jnp.float32
BF16 = jnp.bfloat16
I32 = jnp.int32


def split3(x):
    hi = x.astype(BF16).astype(F32)
    rest = x - hi
    mid = rest.astype(BF16).astype(F32)
    return hi, mid, rest - mid


def dot(a, b):
    return jnp.dot(a, b, preferred_element_type=F32)


def dot_nt(a, b):
    return lax.dot_general(a, b, (((1,), (1,)), ((), ())), preferred_element_type=F32)


def head_kernel(pos, vel, force, mass, feat, slots, w_feat, moved, payload):
    atoms = pos.shape[2]
    m = mass[...]
    parts = [[], [], []]
    for c in range(3):
        half = vel[c] + 0.5 * TIME_STEP * force[c] / m
        new = pos[c] + TIME_STEP * half
        moved[c] = new
        for k, part in enumerate(split3(new)):
            parts[k].append(part)
    rows = parts[0] + parts[1] + parts[2] + [jnp.zeros((PAY - HID - 9, atoms), F32)]
    coords = jnp.concatenate(rows, axis=0).astype(BF16)
    projected = dot(w_feat[...], feat[0]).astype(BF16)
    local = slots[...] & (atoms - 1)
    atom_ids = lax.broadcasted_iota(I32, (atoms, atoms), 0)
    pick = jnp.where(atom_ids == local, 1.0, 0.0).astype(BF16)
    ordered = dot(jnp.concatenate([projected, coords], axis=0), pick).astype(BF16)
    for b in range(atoms // TILE):
        payload[b] = ordered[:, b * TILE : (b + 1) * TILE]


def lane_gather(table, index):
    rows = lax.GatherDimensionNumbers(
        offset_dims=(),
        collapsed_slice_dims=(1,),
        start_index_map=(1,),
        operand_batching_dims=(0,),
        start_indices_batching_dims=(0,),
    )
    return lax.gather(
        table,
        index[..., None],
        rows,
        slice_sizes=(1, 1),
        mode=lax.GatherScatterMode.PROMISE_IN_BOUNDS,
    )


def wrap(c, length):
    return c - length * jnp.floor(c * (1.0 / length) + 0.5)


def pair_kernel(
    blocks_all,
    tiles,
    pos,
    vel,
    force,
    mass,
    slots,
    w_basis,
    bias,
    w_out,
    own,
    one_a,
    one_b,
    two_a,
    two_b,
    moved,
    bead_one,
    bead_two,
    vel_next,
    force_next,
    flat_s,
    proj_s,
    row_s,
    mine_s,
    marks_s,
    list_s,
    lhs_s,
    acc_s,
    index_s,
    geom_s,
    right_s,
    there_s,
    sum_s,
    wout_s,
    count_s,
    rb_s,
    block_s,
    times_s,
    lift_s,
    pass_s,
    pass_rb_s,
    pass_block_s,
):
    atoms = pos.shape[2]
    here = atoms // TILE
    first = lax.axis_index("atom") * here
    depth = blocks_all * LAYER_WIDTH

    for rb in range(here):
        for d in range(DELTAS):
            count_s[rb, d] = 0
        for j in range(DELTAS):
            off = tiles[rb, j] - (first + rb) + REACH
            off = jnp.where(off < 0, off + blocks_all, off)
            off = jnp.where(off >= blocks_all, off - blocks_all, off)
            count_s[rb, off] = count_s[rb, off] + 1

    found = jnp.int32(0)
    split = found
    for rb in range(here):
        if rb == 1:
            split = found
        for d in range(DELTAS):
            times = count_s[rb, d]
            source = first + rb + d - REACH
            rb_s[found] = rb
            block_s[found] = HALO * here + rb + d - REACH
            times_s[found] = times
            lift_s[found] = jnp.where(
                source < 0, depth, jnp.where(source >= blocks_all, -depth, 0.0)
            )
            found = found + jnp.where(times > 0, 1, 0)
    for k in range(BUILD):
        rb_s[found + k] = rb_s[found - 1]
        block_s[found + k] = block_s[found - 1]
        lift_s[found + k] = lift_s[found - 1]
        times_s[found + k] = 0

    place = lax.axis_index("atom")
    side_one = jnp.where((place & 1) == 0, 1, -1)
    side_two = jnp.where((place & 2) == 0, 2, -2)
    sources = ((own, 0), (one_a, side_one), (one_b, -side_one), (two_a, side_two), (two_b, -side_two))
    for ref, away in sources:
        for b in range(here):
            at = (HALO + away) * here + b
            block = ref[b].astype(F32)
            proj_s[at] = block[:HID]
            xyz = block[HID : HID + 3] + block[HID + 3 : HID + 6] + block[HID + 6 : HID + 9]
            plane = xyz[:2]
            plane = plane - SIDE_LENGTH * jnp.floor(plane * (1.0 / SIDE_LENGTH))
            flat_s[at] = jnp.concatenate([plane, xyz[2:], jnp.zeros((5, TILE), F32)], axis=0)

    lane = lax.broadcasted_iota(I32, (SUB, LANES), 1)
    sub = lax.broadcasted_iota(I32, (SUB, LANES), 0)
    group = lane // CAP

    eye = lax.broadcasted_iota(I32, (HID, HID), 0) == lax.broadcasted_iota(I32, (HID, HID), 1)
    bias_parts = split3(jnp.sum(jnp.where(eye, bias[...], 0.0), axis=1, keepdims=True))
    wout_col = jnp.sum(jnp.where(eye, w_out[...], 0.0), axis=1, keepdims=True)
    wout_s[...] = jnp.broadcast_to(wout_col, (HID, LANES))

    depth_k = HID + NB
    col = lax.broadcasted_iota(I32, (HID, depth_k), 1)
    place_r = lax.broadcasted_iota(I32, (NB, depth_k), 0)
    place_c = lax.broadcasted_iota(I32, (NB, depth_k), 1)
    base = dot(w_basis[...], jnp.where(place_r == place_c, 1.0, 0.0).astype(BF16))
    below = dot(w_basis[...], jnp.where(place_r + HID == place_c, 1.0, 0.0).astype(BF16))
    below = below.astype(BF16)
    for k in range(3):
        base = jnp.where(col == NB + GROUPS + k, bias_parts[k], base)
    row_l = lax.broadcasted_iota(I32, (TILE, depth_k), 0)
    col_l = lax.broadcasted_iota(I32, (TILE, depth_k), 1)
    for r in range(SUB):
        sel = (row_l == SUB * (col_l - NB) + r) & (col_l < NB + GROUPS)
        sel = jnp.where(sel, 1.0, 0.0).astype(BF16)
        for rb in range(here):
            lhs_s[rb, r, :HID] = (base + dot(own[rb, :HID, :], sel)).astype(BF16)
            lhs_s[rb, r, HID:] = below

    k_row = lax.broadcasted_iota(I32, (HID - NB, 2 * LANES), 0)
    k_grp = (lax.broadcasted_iota(I32, (HID - NB, 2 * LANES), 1) & (LANES - 1)) // CAP
    fixed = jnp.where((k_row == k_grp) | ((k_row >= GROUPS) & (k_row < GROUPS + 3)), 1.0, 0.0)
    for u in range(UNROLL):
        for r in range(SUB):
            right_s[u, r, NB:HID] = fixed.astype(BF16)

    for rb in range(here):
        own_block = HALO * here + rb
        cols = jnp.transpose(flat_s[own_block])
        for c in range(3):
            row_s[rb, c] = jnp.broadcast_to(cols[:, c : c + 1], (TILE, LANES))
        for c in range(3):
            m = jnp.zeros((SUB, LANES), F32)
            for o in range(GROUPS):
                m = jnp.where(group == o, row_s[rb, c, SUB * o : SUB * (o + 1)], m)
            mine_s[rb, c] = m
            acc_s[rb, c] = jnp.zeros((SUB, 2 * LANES), F32)

    upper = (
        lax.broadcasted_iota(I32, (LANES, LANES), 0) < lax.broadcasted_iota(I32, (LANES, LANES), 1)
    )
    upper = jnp.where(upper, 128.0, 0.0).astype(BF16)
    tag = (lax.broadcasted_iota(I32, (1, LANES), 1) * 129 + 16384).astype(F32)
    inside = CUTOFF * CUTOFF * 1.0001

    def build(k, q):
        rb, block = rb_s[q], block_s[q]
        d2 = None
        for c in range(3):
            there = flat_s[block, c : c + 1, :]
            if c == 2:
                diff = (there - lift_s[q]) - row_s[rb, c]
            else:
                diff = jnp.abs(there - row_s[rb, c])
                diff = jnp.minimum(diff, SIDE_LENGTH - diff)
            d2 = diff * diff if d2 is None else d2 + diff * diff
        near = d2 < inside
        mask = jnp.where(near, 1.0, 0.0)
        rank = dot(mask.astype(BF16), upper)
        fullest = jnp.max(rank + 128.0 * mask).astype(I32)
        marks_s[k] = jnp.where(near, tag - rank, 0.0).astype(I32)
        passes = jnp.maximum((fullest + (128 * CAP - 1)) // (128 * CAP), 1)
        pass_s[q] = passes
        return passes

    def compact(k, q):
        v = marks_s[k].astype(jnp.int16)
        for bit in range(7):
            go = jnp.where((v & jnp.int16(128 << bit)) != jnp.int16(0), v, jnp.int16(0))
            v = (v ^ go) | pltpu.roll(go, LANES - (1 << bit), 1)
        v = v.astype(I32)
        for o in range(GROUPS):
            piece = v[SUB * o : SUB * (o + 1)]
            list_s[q, o] = piece if o == 0 else pltpu.roll(piece, CAP * o, 1)

    def build_some(i, totals):
        low, all_of = totals
        for k in range(BUILD):
            compact(k, jnp.where(i > 0, BUILD * (i - 1) + k, here * DELTAS + BUILD))
        for k in range(BUILD):
            q = jnp.minimum(BUILD * i + k, found)
            passes = jnp.where(q < found, build(k, q), 0)
            low = low + jnp.where(rb_s[q] == 0, passes, 0)
            all_of = all_of + passes
        return low, all_of

    for k in range(BUILD):
        marks_s[k] = jnp.zeros((TILE, LANES), I32)
    low, total = lax.fori_loop(0, (found + BUILD - 1) // BUILD + 1, build_some, (jnp.int32(0), jnp.int32(0)))
    odd = low & 1
    pass_s[split - 1] = pass_s[split - 1] + odd
    pairs = (total + odd + 1) // 2

    sharp = (BASIS_SHARPNESS * 1.4426950408889634) ** 0.5
    centre = (lax.broadcasted_iota(I32, (NB, 1), 0).astype(F32) + 0.5) * (CUTOFF / NB * sharp)

    def front(q, p, i, side):
        rb, block = rb_s[q], block_s[q]
        half = slice(LANES * side, LANES * (side + 1))
        pass_rb_s[i] = rb
        pass_block_s[i, side] = block
        times = jnp.where(p < GROUPS, times_s[q].astype(F32) * 2.0, 0.0)
        which = jnp.minimum(q, found - 1)
        here_group = (group - p) & (GROUPS - 1)
        level = [list_s[which, o] for o in range(GROUPS)]
        bit = 1
        while len(level) > 1:
            choose = (here_group & bit) != 0
            level = [
                jnp.where(choose, level[2 * k + 1], level[2 * k]) for k in range(len(level) // 2)
            ]
            bit *= 2
        slot = pltpu.roll(level[0], (LANES - CAP * p) & (LANES - 1), 1)
        idx = slot & (LANES - 1)
        index_s[i, :, half] = idx
        weight = jnp.where(slot >= 16384, times, 0.0)
        d2 = None
        for c in range(3):
            table = jnp.broadcast_to(flat_s[block, c : c + 1, :], (SUB, LANES))
            there = jnp.take_along_axis(table, idx, axis=1, mode="promise_in_bounds")
            one = there - mine_s[rb, c]
            one = one - lift_s[q] if c == 2 else wrap(one, SIDE_LENGTH)
            geom_s[i, c, :, half] = one
            d2 = one * one if d2 is None else d2 + one * one
        distance = jnp.sqrt(d2 + SOFTEN)
        inner_part = jnp.maximum(1.0 - d2 * (1.0 / (CUTOFF * CUTOFF)), 0.0)
        weight = weight * inner_part
        geom_s[i, 3, :, half] = distance * sharp
        geom_s[i, 4, :, half] = weight * inner_part * ((-BASIS_SHARPNESS / sharp) / distance)
        geom_s[i, 5, :, half] = weight * (-2.0 / (CUTOFF * CUTOFF))

    def advance(q, p):
        last = p + 1 >= pass_s[q]
        return jnp.where(last, q + 1, q), jnp.where(last, 0, p + 1)

    pass_s[found] = 1 << 20

    def front_some(i, state):
        q, p = state
        for k in range(2 * UNROLL):
            front(q, p, i * UNROLL + k // 2, k % 2)
            q, p = advance(q, p)
        return q, p

    turns = (pairs + (UNROLL - 1)) // UNROLL
    lax.fori_loop(0, turns, front_some, (jnp.int32(0), jnp.int32(0)))

    def first_half(i, u, r):
        offset = geom_s[i, 3, r : r + 1, :] - centre
        basis = jnp.exp2(-(offset * offset))
        right_s[u, r, 0:NB] = basis.astype(BF16)
        right_s[u, r, HID : HID + NB] = (offset * basis).astype(BF16)
        for side in range(2):
            half = slice(LANES * side, LANES * (side + 1))
            at = jnp.broadcast_to(index_s[i, r : r + 1, half], (HID, LANES))
            there_s[u, r, :, half] = lane_gather(proj_s[pass_block_s[i, side]], at)

    def fold(x):
        part = x[0:SUB]
        for k in range(1, x.shape[0] // SUB):
            part = part + x[SUB * k : SUB * (k + 1)]
        return part

    def second_half(i, u, r):
        both = dot(lhs_s[pass_rb_s[i], r], right_s[u, r])
        act = jnp.tanh(both[:HID] + there_s[u, r])
        w_o = wout_s[...]
        w_o = jnp.concatenate([w_o, w_o], axis=1)
        share = w_o * act
        energy = fold(share)
        grad = fold((w_o - share * act) * both[HID:])
        for side in range(2):
            half = slice(LANES * side, LANES * (side + 1))
            sum_s[u, side, SUB * r : SUB * (r + 1)] = energy[:, half]
            sum_s[u, 2 + side, SUB * r : SUB * (r + 1)] = grad[:, half]

    def last_part(i, u):
        sums = []
        for k in range(4):
            one = sum_s[u, k, pl.ds(0, SUB, stride=SUB)]
            for j in range(1, SUB):
                one = one + sum_s[u, k, pl.ds(j, SUB, stride=SUB)]
            sums.append(one)
        energy = jnp.concatenate(sums[:2], axis=1)
        grad = jnp.concatenate(sums[2:], axis=1)
        coef = geom_s[i, 5] * energy + geom_s[i, 4] * grad
        rb = pass_rb_s[i]
        for c in range(3):
            acc_s[rb, c] = acc_s[rb, c] + coef * geom_s[i, c]

    def step(i, carry):
        for u in range(UNROLL):
            for r in range(SUB):
                first_half(UNROLL * i + u, u, r)
                second_half(UNROLL * i + u, u, r)
        for u in range(UNROLL):
            last_part(UNROLL * i + u, u)
        return carry

    lax.fori_loop(0, turns, step, 0)

    forces = []
    for rb in range(here):
        rows = []
        for c in range(3):
            a = acc_s[rb, c, :, :LANES] + acc_s[rb, c, :, LANES:]
            for step in (1, 2, 4):
                down = pltpu.roll(a, LANES - step, 1)
                up = pltpu.roll(a, step, 1)
                a = a + jnp.where((lane & step) == 0, down, up)
            a = jnp.where((lane & (CAP - 1)) == sub, a, 0.0)
            rows.append(jnp.sum(a, axis=0, keepdims=True))
        forces.append(rows)

    full = [jnp.concatenate([forces[rb][c] for rb in range(here)], axis=1) for c in range(3)]
    parts = [split3(f) for f in full]
    stacked = [parts[c][k] for k in range(3) for c in range(3)]
    stacked = jnp.concatenate(stacked + [jnp.zeros((7, atoms), F32)], axis=0).astype(BF16)
    local = slots[...] & (atoms - 1)
    atom_ids = lax.broadcasted_iota(I32, (atoms, atoms), 0)
    pick = jnp.where(atom_ids == local, 1.0, 0.0).astype(BF16)
    placed = dot_nt(stacked, pick)
    m = mass[...]
    for c in range(3):
        pair = placed[c : c + 1] + placed[3 + c : 4 + c] + placed[6 + c : 7 + c]
        half = vel[c] + 0.5 * TIME_STEP * force[c] / m
        spring = -OMEGA_SQ * m * (2.0 * moved[c] - bead_one[c] - bead_two[c])
        total_force = pair + spring
        force_next[c] = total_force
        vel_next[c] = half + 0.5 * TIME_STEP * total_force / m


def swapped(block, axis, step, other):
    count = lax.axis_size(axis)
    route = []
    for i in range(count):
        up = ((i // step) % 2 == 0) != other
        route.append((i, (i + step if up else i - step) % count))
    return lax.ppermute(block, axis, route)


def body(
    positions,
    velocities,
    forces_now,
    masses,
    features,
    tile_blocks,
    block_slots,
    w_basis,
    w_feat,
    hidden_bias,
    w_out,
):
    atoms = positions.shape[2]
    here = atoms // TILE
    blocks_all = here * lax.axis_size("atom")
    mass = masses.reshape(1, atoms)
    slots = block_slots.reshape(1, atoms)
    moved, payload = pl.pallas_call(
        head_kernel,
        out_shape=(
            jax.ShapeDtypeStruct(positions.shape, F32),
            jax.ShapeDtypeStruct((here, PAY, TILE), BF16),
        ),
        name="head",
    )(positions, velocities, forces_now, mass, features, slots, w_feat)
    bead_one = swapped(moved, "bead", 1, False)
    bead_two = swapped(moved, "bead", 1, True)
    near = [swapped(payload, "atom", step, other) for step in (1, 2) for other in (False, True)]
    vmem = pl.BlockSpec(memory_space=pltpu.VMEM)
    sources = 2 * HALO + 1
    room = here * DELTAS * GROUPS // 2 + 16
    vel_next, force_next = pl.pallas_call(
        functools.partial(pair_kernel, blocks_all),
        out_shape=(
            jax.ShapeDtypeStruct(positions.shape, F32),
            jax.ShapeDtypeStruct(positions.shape, F32),
        ),
        in_specs=[pl.BlockSpec(memory_space=pltpu.SMEM)] + [vmem] * 16,
        out_specs=(vmem, vmem),
        scratch_shapes=[
            pltpu.VMEM((sources * here, SUB, TILE), F32),
            pltpu.VMEM((sources * here, HID, TILE), F32),
            pltpu.VMEM((here, 3, TILE, LANES), F32),
            pltpu.VMEM((here, 3, SUB, LANES), F32),
            pltpu.VMEM((BUILD, TILE, LANES), I32),
            pltpu.VMEM((here * DELTAS + BUILD + 1, GROUPS, SUB, LANES), I32),
            pltpu.VMEM((here, SUB, 2 * HID, HID + NB), BF16),
            pltpu.VMEM((here, 3, SUB, 2 * LANES), F32),
            pltpu.VMEM((room, SUB, 2 * LANES), I32),
            pltpu.VMEM((room, 6, SUB, 2 * LANES), F32),
            pltpu.VMEM((UNROLL, SUB, HID + NB, 2 * LANES), BF16),
            pltpu.VMEM((UNROLL, SUB, HID, 2 * LANES), F32),
            pltpu.VMEM((UNROLL, 4, SUB * SUB, LANES), F32),
            pltpu.VMEM((HID, LANES), F32),
            pltpu.SMEM((here, DELTAS), I32),
            pltpu.SMEM((here * DELTAS + BUILD,), I32),
            pltpu.SMEM((here * DELTAS + BUILD,), I32),
            pltpu.SMEM((here * DELTAS + BUILD,), I32),
            pltpu.SMEM((here * DELTAS + BUILD,), F32),
            pltpu.SMEM((here * DELTAS + BUILD,), I32),
            pltpu.SMEM((room,), I32),
            pltpu.SMEM((room, 2), I32),
        ],
        name="pairs",
    )(
        tile_blocks,
        positions,
        velocities,
        forces_now,
        mass,
        slots,
        w_basis,
        hidden_bias.reshape(1, HID),
        w_out.reshape(1, HID),
        payload,
        *near,
        moved,
        bead_one,
        bead_two,
    )
    return (moved, vel_next, force_next)


def solution(mesh):
    return jax.shard_map(
        body,
        mesh=mesh,
        in_specs=(
            P(None, "bead", "atom"),
            P(None, "bead", "atom"),
            P(None, "bead", "atom"),
            P("atom"),
            P("bead", None, "atom"),
            P("atom", None),
            P("atom"),
            P(),
            P(),
            P(),
            P(),
        ),
        out_specs=(P(None, "bead", "atom"), P(None, "bead", "atom"), P(None, "bead", "atom")),
        check_vma=False,
    )
```

```python
import functools

import jax
import jax.numpy as jnp
from jax import lax
from jax.experimental import pallas as pl
from jax.experimental.pallas import tpu as pltpu
from jax.sharding import PartitionSpec as P

TILE = 128
NB = 32
HID = 64
LANES = 128
SUB = 8
CAP = 8
GROUPS = LANES // CAP
PAY = 80
UNROLL = 3
BUILD = 2
HALO = 2
REACH = 4
DELTAS = 2 * REACH + 1

LAYER_WIDTH = 0.15
SIDE_LENGTH = 2.9
CUTOFF = 0.6
BASIS_SHARPNESS = 355.0
SOFTEN = 0.0001
TIME_STEP = 0.1
OMEGA_SQ = 100.0

F32 = jnp.float32
BF16 = jnp.bfloat16
I32 = jnp.int32


def split3(x):
    hi = x.astype(BF16).astype(F32)
    rest = x - hi
    mid = rest.astype(BF16).astype(F32)
    return hi, mid, rest - mid


def dot(a, b):
    return jnp.dot(a, b, preferred_element_type=F32)


def dot_nt(a, b):
    return lax.dot_general(a, b, (((1,), (1,)), ((), ())), preferred_element_type=F32)


def head_kernel(
    blocks_all,
    tiles,
    pos,
    vel,
    force,
    mass,
    feat,
    slots,
    w_feat,
    w_basis_t,
    bias,
    w_out,
    moved,
    payload,
    moved_v,
    half_v,
    mass_v,
    slots_v,
    w_basis_v,
    bias_v,
    w_out_v,
    count,
):
    atoms = pos.shape[2]
    here = atoms // TILE
    m = mass[...]
    parts = [[], [], []]
    for c in range(3):
        half = vel[c] + 0.5 * TIME_STEP * force[c] / m
        new = pos[c] + TIME_STEP * half
        moved[c] = new
        moved_v[c] = new
        half_v[c] = half
        for k, part in enumerate(split3(new)):
            parts[k].append(part)
    rows = parts[0] + parts[1] + parts[2] + [jnp.zeros((PAY - HID - 9, atoms), F32)]
    coords = jnp.concatenate(rows, axis=0).astype(BF16)
    projected = dot(w_feat[...], feat[0]).astype(BF16)
    local = slots[...] & (atoms - 1)
    atom_ids = lax.broadcasted_iota(I32, (atoms, atoms), 0)
    pick = jnp.where(atom_ids == local, 1.0, 0.0).astype(BF16)
    ordered = dot(jnp.concatenate([projected, coords], axis=0), pick).astype(BF16)
    for b in range(here):
        payload[b] = ordered[:, b * TILE : (b + 1) * TILE]
    mass_v[...] = m
    slots_v[...] = local
    w_basis_v[...] = w_basis_t[...]
    bias_v[...] = bias[...]
    w_out_v[...] = w_out[...]
    first = lax.axis_index("atom") * here
    for rb in range(here):
        for d in range(DELTAS):
            count[rb, d] = 0
        for j in range(DELTAS):
            off = tiles[rb, j] - (first + rb) + REACH
            off = jnp.where(off < 0, off + blocks_all, off)
            off = jnp.where(off >= blocks_all, off - blocks_all, off)
            count[rb, off] = count[rb, off] + 1


def lane_gather(table, index):
    rows = lax.GatherDimensionNumbers(
        offset_dims=(),
        collapsed_slice_dims=(1,),
        start_index_map=(1,),
        operand_batching_dims=(0,),
        start_indices_batching_dims=(0,),
    )
    return lax.gather(
        table,
        index[..., None],
        rows,
        slice_sizes=(1, 1),
        mode=lax.GatherScatterMode.PROMISE_IN_BOUNDS,
    )


def wrap(c, length):
    return c - length * jnp.floor(c * (1.0 / length) + 0.5)


def load_block(ref, b, at, flat_s, proj_s):
    block = ref[b].astype(F32)
    proj_s[at] = block[:HID]
    xyz = block[HID : HID + 3] + block[HID + 3 : HID + 6] + block[HID + 6 : HID + 9]
    plane = xyz[:2]
    plane = plane - SIDE_LENGTH * jnp.floor(plane * (1.0 / SIDE_LENGTH))
    flat_s[at] = jnp.concatenate([plane, xyz[2:], jnp.zeros((5, TILE), F32)], axis=0)


def visit_tiles(local, blocks_all, here, count_s, row_s, mine_s, lhs_s, wout_s, acc_s, scratch):
    (
        flat_s,
        proj_s,
        marks_s,
        list_s,
        index_s,
        geom_s,
        right_s,
        there_s,
        sum_s,
        rb_s,
        block_s,
        times_s,
        lift_s,
        pass_s,
        pass_rb_s,
        pass_block_s,
    ) = scratch
    first = lax.axis_index("atom") * here
    depth = blocks_all * LAYER_WIDTH
    lane = lax.broadcasted_iota(I32, (SUB, LANES), 1)
    group = lane // CAP

    found = jnp.int32(0)
    split = found
    for rb in range(here):
        if rb == 1:
            split = found
        for d in range(DELTAS):
            if (0 <= rb + d - REACH < here) != local:
                continue
            times = count_s[rb, d]
            source = first + rb + d - REACH
            rb_s[found] = rb
            block_s[found] = HALO * here + rb + d - REACH
            times_s[found] = times
            lift_s[found] = jnp.where(
                source < 0, depth, jnp.where(source >= blocks_all, -depth, 0.0)
            )
            found = found + jnp.where(times > 0, 1, 0)
    last = jnp.maximum(found - 1, 0)
    for k in range(BUILD):
        rb_s[found + k] = rb_s[last]
        block_s[found + k] = block_s[last]
        lift_s[found + k] = lift_s[last]
        times_s[found + k] = 0

    k_row = lax.broadcasted_iota(I32, (HID - NB, 2 * LANES), 0)
    k_grp = (lax.broadcasted_iota(I32, (HID - NB, 2 * LANES), 1) & (LANES - 1)) // CAP
    fixed = jnp.where((k_row == k_grp) | ((k_row >= GROUPS) & (k_row < GROUPS + 3)), 1.0, 0.0)
    for u in range(UNROLL):
        for r in range(SUB):
            right_s[u, r, NB:HID] = fixed.astype(BF16)

    upper = (
        lax.broadcasted_iota(I32, (LANES, LANES), 0) < lax.broadcasted_iota(I32, (LANES, LANES), 1)
    )
    upper = jnp.where(upper, 128.0, 0.0).astype(BF16)
    tag = (lax.broadcasted_iota(I32, (1, LANES), 1) * 129 + 16384).astype(F32)
    inside = CUTOFF * CUTOFF * 1.0001

    def build(k, q):
        rb, block = rb_s[q], block_s[q]
        d2 = None
        for c in range(3):
            there = flat_s[block, c : c + 1, :]
            if c == 2:
                diff = (there - lift_s[q]) - row_s[rb, c]
            else:
                diff = jnp.abs(there - row_s[rb, c])
                diff = jnp.minimum(diff, SIDE_LENGTH - diff)
            d2 = diff * diff if d2 is None else d2 + diff * diff
        near = d2 < inside
        mask = jnp.where(near, 1.0, 0.0)
        rank = dot(mask.astype(BF16), upper)
        fullest = jnp.max(rank + 128.0 * mask).astype(I32)
        marks_s[k] = jnp.where(near, tag - rank, 0.0).astype(I32)
        passes = jnp.maximum((fullest + (128 * CAP - 1)) // (128 * CAP), 1)
        pass_s[q] = passes
        return passes

    def compact(k, q):
        v = marks_s[k].astype(jnp.int16)
        for bit in range(7):
            go = jnp.where((v & jnp.int16(128 << bit)) != jnp.int16(0), v, jnp.int16(0))
            v = (v ^ go) | pltpu.roll(go, LANES - (1 << bit), 1)
        v = v.astype(I32)
        for o in range(GROUPS):
            piece = v[SUB * o : SUB * (o + 1)]
            list_s[q, o] = piece if o == 0 else pltpu.roll(piece, CAP * o, 1)

    def build_some(i, totals):
        low, all_of = totals
        for k in range(BUILD):
            compact(k, jnp.where(i > 0, BUILD * (i - 1) + k, here * DELTAS + BUILD))
        for k in range(BUILD):
            q = jnp.minimum(BUILD * i + k, found)
            passes = jnp.where(q < found, build(k, q), 0)
            low = low + jnp.where(rb_s[q] == 0, passes, 0)
            all_of = all_of + passes
        return low, all_of

    for k in range(BUILD):
        marks_s[k] = jnp.zeros((TILE, LANES), I32)
    low, total = lax.fori_loop(0, (found + BUILD - 1) // BUILD + 1, build_some, (jnp.int32(0), jnp.int32(0)))
    odd = low & 1
    before = jnp.maximum(split - 1, 0)
    pass_s[before] = pass_s[before] + odd
    pairs = (total + odd + 1) // 2

    sharp = (BASIS_SHARPNESS * 1.4426950408889634) ** 0.5
    centre = (lax.broadcasted_iota(I32, (NB, 1), 0).astype(F32) + 0.5) * (CUTOFF / NB * sharp)

    def front(q, p, i, side):
        rb, block = rb_s[q], block_s[q]
        half = slice(LANES * side, LANES * (side + 1))
        pass_rb_s[i] = rb
        pass_block_s[i, side] = block
        times = jnp.where(p < GROUPS, times_s[q].astype(F32) * 2.0, 0.0)
        which = jnp.minimum(q, found - 1)
        here_group = (group - p) & (GROUPS - 1)
        level = [list_s[which, o] for o in range(GROUPS)]
        bit = 1
        while len(level) > 1:
            choose = (here_group & bit) != 0
            level = [
                jnp.where(choose, level[2 * k + 1], level[2 * k]) for k in range(len(level) // 2)
            ]
            bit *= 2
        slot = pltpu.roll(level[0], (LANES - CAP * p) & (LANES - 1), 1)
        idx = slot & (LANES - 1)
        index_s[i, :, half] = idx
        weight = jnp.where(slot >= 16384, times, 0.0)
        d2 = None
        for c in range(3):
            table = jnp.broadcast_to(flat_s[block, c : c + 1, :], (SUB, LANES))
            there = jnp.take_along_axis(table, idx, axis=1, mode="promise_in_bounds")
            one = there - mine_s[rb, c]
            one = one - lift_s[q] if c == 2 else wrap(one, SIDE_LENGTH)
            geom_s[i, c, :, half] = one
            d2 = one * one if d2 is None else d2 + one * one
        distance = jnp.sqrt(d2 + SOFTEN)
        inner_part = jnp.maximum(1.0 - d2 * (1.0 / (CUTOFF * CUTOFF)), 0.0)
        weight = weight * inner_part
        geom_s[i, 3, :, half] = distance * sharp
        geom_s[i, 4, :, half] = weight * inner_part * ((-BASIS_SHARPNESS / sharp) / distance)
        geom_s[i, 5, :, half] = weight * (-2.0 / (CUTOFF * CUTOFF))

    def advance(q, p):
        last = p + 1 >= pass_s[q]
        return jnp.where(last, q + 1, q), jnp.where(last, 0, p + 1)

    pass_s[found] = 1 << 20

    def front_some(i, state):
        q, p = state
        for k in range(2 * UNROLL):
            front(q, p, i * UNROLL + k // 2, k % 2)
            q, p = advance(q, p)
        return q, p

    turns = (pairs + (UNROLL - 1)) // UNROLL
    lax.fori_loop(0, turns, front_some, (jnp.int32(0), jnp.int32(0)))

    def first_half(i, u, r):
        offset = geom_s[i, 3, r : r + 1, :] - centre
        basis = jnp.exp2(-(offset * offset))
        right_s[u, r, 0:NB] = basis.astype(BF16)
        right_s[u, r, HID : HID + NB] = (offset * basis).astype(BF16)
        for side in range(2):
            half = slice(LANES * side, LANES * (side + 1))
            at = jnp.broadcast_to(index_s[i, r : r + 1, half], (HID, LANES))
            there_s[u, r, :, half] = lane_gather(proj_s[pass_block_s[i, side]], at)

    def fold(x):
        part = x[0:SUB]
        for k in range(1, x.shape[0] // SUB):
            part = part + x[SUB * k : SUB * (k + 1)]
        return part

    def second_half(i, u, r):
        both = dot(lhs_s[pass_rb_s[i], r], right_s[u, r])
        act = jnp.tanh(both[:HID] + there_s[u, r])
        w_o = wout_s[...]
        w_o = jnp.concatenate([w_o, w_o], axis=1)
        share = w_o * act
        energy = fold(share)
        grad = fold((w_o - share * act) * both[HID:])
        for side in range(2):
            half = slice(LANES * side, LANES * (side + 1))
            sum_s[u, side, SUB * r : SUB * (r + 1)] = energy[:, half]
            sum_s[u, 2 + side, SUB * r : SUB * (r + 1)] = grad[:, half]

    def last_part(i, u):
        sums = []
        for k in range(4):
            one = sum_s[u, k, pl.ds(0, SUB, stride=SUB)]
            for j in range(1, SUB):
                one = one + sum_s[u, k, pl.ds(j, SUB, stride=SUB)]
            sums.append(one)
        energy = jnp.concatenate(sums[:2], axis=1)
        grad = jnp.concatenate(sums[2:], axis=1)
        coef = geom_s[i, 5] * energy + geom_s[i, 4] * grad
        rb = pass_rb_s[i]
        for c in range(3):
            acc_s[rb, c] = acc_s[rb, c] + coef * geom_s[i, c]

    def step(i, carry):
        for u in range(UNROLL):
            for r in range(SUB):
                first_half(UNROLL * i + u, u, r)
                second_half(UNROLL * i + u, u, r)
        for u in range(UNROLL):
            last_part(UNROLL * i + u, u)
        return carry

    lax.fori_loop(0, turns, step, 0)


def local_kernel(
    blocks_all, count, w_basis_t, bias, w_out, own, acc_s, row_s, mine_s, lhs_s, wout_s, *scratch
):
    here = own.shape[0]
    flat_s, proj_s = scratch[:2]
    lane = lax.broadcasted_iota(I32, (SUB, LANES), 1)
    group = lane // CAP
    for b in range(here):
        load_block(own, b, HALO * here + b, flat_s, proj_s)

    w_basis = jnp.transpose(w_basis_t[...].astype(F32)).astype(BF16)
    eye = lax.broadcasted_iota(I32, (HID, HID), 0) == lax.broadcasted_iota(I32, (HID, HID), 1)
    bias_parts = split3(jnp.sum(jnp.where(eye, bias[...], 0.0), axis=1, keepdims=True))
    wout_col = jnp.sum(jnp.where(eye, w_out[...], 0.0), axis=1, keepdims=True)
    wout_s[...] = jnp.broadcast_to(wout_col, (HID, LANES))

    depth_k = HID + NB
    col = lax.broadcasted_iota(I32, (HID, depth_k), 1)
    place_r = lax.broadcasted_iota(I32, (NB, depth_k), 0)
    place_c = lax.broadcasted_iota(I32, (NB, depth_k), 1)
    base = dot(w_basis, jnp.where(place_r == place_c, 1.0, 0.0).astype(BF16))
    below = dot(w_basis, jnp.where(place_r + HID == place_c, 1.0, 0.0).astype(BF16))
    below = below.astype(BF16)
    for k in range(3):
        base = jnp.where(col == NB + GROUPS + k, bias_parts[k], base)
    row_l = lax.broadcasted_iota(I32, (TILE, depth_k), 0)
    col_l = lax.broadcasted_iota(I32, (TILE, depth_k), 1)
    for r in range(SUB):
        sel = (row_l == SUB * (col_l - NB) + r) & (col_l < NB + GROUPS)
        sel = jnp.where(sel, 1.0, 0.0).astype(BF16)
        for rb in range(here):
            lhs_s[rb, r, :HID] = (base + dot(own[rb, :HID, :], sel)).astype(BF16)
            lhs_s[rb, r, HID:] = below

    for rb in range(here):
        own_block = HALO * here + rb
        cols = jnp.transpose(flat_s[own_block])
        for c in range(3):
            row_s[rb, c] = jnp.broadcast_to(cols[:, c : c + 1], (TILE, LANES))
        for c in range(3):
            m = jnp.zeros((SUB, LANES), F32)
            for o in range(GROUPS):
                m = jnp.where(group == o, row_s[rb, c, SUB * o : SUB * (o + 1)], m)
            mine_s[rb, c] = m
            acc_s[rb, c] = jnp.zeros((SUB, 2 * LANES), F32)

    visit_tiles(True, blocks_all, here, count, row_s, mine_s, lhs_s, wout_s, acc_s, scratch)


def far_kernel(
    blocks_all,
    count,
    half,
    mass,
    slots,
    one_a,
    one_b,
    two_a,
    two_b,
    moved,
    bead_one,
    bead_two,
    acc_local,
    row_s,
    mine_s,
    lhs_s,
    wout_s,
    vel_next,
    force_next,
    acc_s,
    *scratch,
):
    atoms = half.shape[2]
    here = atoms // TILE
    flat_s, proj_s = scratch[:2]
    lane = lax.broadcasted_iota(I32, (SUB, LANES), 1)
    sub = lax.broadcasted_iota(I32, (SUB, LANES), 0)
    acc_s[...] = acc_local[...]
    place = lax.axis_index("atom")
    side_one = jnp.where((place & 1) == 0, 1, -1)
    side_two = jnp.where((place & 2) == 0, 2, -2)
    sources = ((one_a, side_one), (one_b, -side_one), (two_a, side_two), (two_b, -side_two))
    for ref, away in sources:
        for b in range(here):
            at = (HALO + away) * here + b
            load_block(ref, b, at, flat_s, proj_s)

    visit_tiles(False, blocks_all, here, count, row_s, mine_s, lhs_s, wout_s, acc_s, scratch)

    forces = []
    for rb in range(here):
        rows = []
        for c in range(3):
            a = acc_s[rb, c, :, :LANES] + acc_s[rb, c, :, LANES:]
            for step in (1, 2, 4):
                down = pltpu.roll(a, LANES - step, 1)
                up = pltpu.roll(a, step, 1)
                a = a + jnp.where((lane & step) == 0, down, up)
            a = jnp.where((lane & (CAP - 1)) == sub, a, 0.0)
            rows.append(jnp.sum(a, axis=0, keepdims=True))
        forces.append(rows)

    full = [jnp.concatenate([forces[rb][c] for rb in range(here)], axis=1) for c in range(3)]
    parts = [split3(f) for f in full]
    stacked = [parts[c][k] for k in range(3) for c in range(3)]
    stacked = jnp.concatenate(stacked + [jnp.zeros((7, atoms), F32)], axis=0).astype(BF16)
    atom_ids = lax.broadcasted_iota(I32, (atoms, atoms), 0)
    pick = jnp.where(atom_ids == slots[...], 1.0, 0.0).astype(BF16)
    placed = dot_nt(stacked, pick)
    m = mass[...]
    for c in range(3):
        pair = placed[c : c + 1] + placed[3 + c : 4 + c] + placed[6 + c : 7 + c]
        spring = -OMEGA_SQ * m * (2.0 * moved[c] - bead_one[c] - bead_two[c])
        total_force = pair + spring
        force_next[c] = total_force
        vel_next[c] = half[c] + 0.5 * TIME_STEP * total_force / m


def in_vmem(x):
    return pltpu.with_memory_space_constraint(x, pltpu.VMEM)


def in_smem(x):
    return pltpu.with_memory_space_constraint(x, pltpu.SMEM)


def swapped(block, axis, step, other):
    count = lax.axis_size(axis)
    route = []
    for i in range(count):
        up = ((i // step) % 2 == 0) != other
        route.append((i, (i + step if up else i - step) % count))
    return lax.ppermute(block, axis, route)


def body(
    positions,
    velocities,
    forces_now,
    masses,
    features,
    tile_blocks,
    block_slots,
    w_basis,
    w_feat,
    hidden_bias,
    w_out,
):
    atoms = positions.shape[2]
    here = atoms // TILE
    blocks_all = here * lax.axis_size("atom")
    mass = masses.reshape(1, atoms)
    slots = block_slots.reshape(1, atoms)
    vmem = pl.BlockSpec(memory_space=pltpu.VMEM)
    smem = pl.BlockSpec(memory_space=pltpu.SMEM)
    moved, payload, moved_v, half, mass_v, slots_v, w_basis_v, bias_v, w_out_v, count = pl.pallas_call(
        functools.partial(head_kernel, blocks_all),
        out_shape=(
            jax.ShapeDtypeStruct(positions.shape, F32),
            pltpu.VMEM((here, PAY, TILE), BF16),
            pltpu.VMEM(positions.shape, F32),
            pltpu.VMEM(positions.shape, F32),
            pltpu.VMEM((1, atoms), F32),
            pltpu.VMEM((1, atoms), I32),
            pltpu.VMEM((NB, HID), BF16),
            pltpu.VMEM((1, HID), F32),
            pltpu.VMEM((1, HID), F32),
            pltpu.SMEM((here, DELTAS), I32),
        ),
        in_specs=[smem] + [vmem] * 10,
        out_specs=(vmem,) * 9 + (smem,),
        name="head",
    )(
        tile_blocks,
        positions,
        velocities,
        forces_now,
        mass,
        features,
        slots,
        w_feat,
        w_basis.T,
        hidden_bias.reshape(1, HID),
        w_out.reshape(1, HID),
    )
    bead_one = swapped(moved_v, "bead", 1, False)
    bead_two = swapped(moved_v, "bead", 1, True)
    near = [swapped(payload, "atom", step, other) for step in (1, 2) for other in (False, True)]
    sources = 2 * HALO + 1

    tile_room = here * DELTAS
    room = tile_room * GROUPS // 2 + 16
    scratch = [
            pltpu.VMEM((sources * here, SUB, TILE), F32),
            pltpu.VMEM((sources * here, HID, TILE), F32),
            pltpu.VMEM((BUILD, TILE, LANES), I32),
            pltpu.VMEM((tile_room + BUILD + 1, GROUPS, SUB, LANES), I32),
            pltpu.VMEM((room, SUB, 2 * LANES), I32),
            pltpu.VMEM((room, 6, SUB, 2 * LANES), F32),
            pltpu.VMEM((UNROLL, SUB, HID + NB, 2 * LANES), BF16),
            pltpu.VMEM((UNROLL, SUB, HID, 2 * LANES), F32),
            pltpu.VMEM((UNROLL, 4, SUB * SUB, LANES), F32),
            pltpu.SMEM((tile_room + BUILD,), I32),
            pltpu.SMEM((tile_room + BUILD,), I32),
            pltpu.SMEM((tile_room + BUILD,), I32),
            pltpu.SMEM((tile_room + BUILD,), F32),
            pltpu.SMEM((tile_room + BUILD,), I32),
            pltpu.SMEM((room,), I32),
            pltpu.SMEM((room, 2), I32),
        ]

    acc_shape = (here, 3, SUB, 2 * LANES)
    tables = pl.pallas_call(
        functools.partial(local_kernel, blocks_all),
        out_shape=(
            pltpu.VMEM(acc_shape, F32),
            pltpu.VMEM((here, 3, TILE, LANES), F32),
            pltpu.VMEM((here, 3, SUB, LANES), F32),
            pltpu.VMEM((here, SUB, 2 * HID, HID + NB), BF16),
            pltpu.VMEM((HID, LANES), F32),
        ),
        in_specs=[smem] + [vmem] * 4,
        out_specs=(vmem,) * 5,
        scratch_shapes=scratch,
        cost_estimate=pl.CostEstimate(flops=3_000_000_000, bytes_accessed=2_000_000, transcendentals=0),
        name="near",
    )(in_smem(count), *(in_vmem(x) for x in (w_basis_v, bias_v, w_out_v, payload)))
    vel_next, force_next = pl.pallas_call(
        functools.partial(far_kernel, blocks_all),
        out_shape=(
            jax.ShapeDtypeStruct(positions.shape, F32),
            jax.ShapeDtypeStruct(positions.shape, F32),
        ),
        in_specs=[smem] + [vmem] * 15,
        out_specs=(vmem, vmem),
        scratch_shapes=[pltpu.VMEM(acc_shape, F32)] + scratch,
        name="far",
    )(
        in_smem(count),
        *(in_vmem(x) for x in (half, mass_v, slots_v, *near)),
        *(in_vmem(x) for x in (moved_v, bead_one, bead_two, *tables)),
    )
    return (moved, vel_next, force_next)


def solution(mesh):
    return jax.shard_map(
        body,
        mesh=mesh,
        in_specs=(
            P(None, "bead", "atom"),
            P(None, "bead", "atom"),
            P(None, "bead", "atom"),
            P("atom"),
            P("bead", None, "atom"),
            P("atom", None),
            P("atom"),
            P(),
            P(),
            P(),
            P(),
        ),
        out_specs=(P(None, "bead", "atom"), P(None, "bead", "atom"), P(None, "bead", "atom")),
        check_vma=False,
    )
```

```python
import functools

import jax
import jax.numpy as jnp
from jax import lax
from jax.experimental import pallas as pl
from jax.experimental.pallas import tpu as pltpu
from jax.sharding import PartitionSpec as P


TILE = 128
NB = 32
HID = 64
LANES = 128
SUB = 8
CAP = 8
GROUPS = LANES // CAP
PAY = 80
UNROLL = 3
BUILD = 2
HALO = 2
REACH = 4
DELTAS = 2 * REACH + 1

LAYER_WIDTH = 0.15
SIDE_LENGTH = 2.9
CUTOFF = 0.6
BASIS_SHARPNESS = 355.0
SOFTEN = 0.0001
TIME_STEP = 0.1
OMEGA_SQ = 100.0

F32 = jnp.float32
BF16 = jnp.bfloat16
I32 = jnp.int32


def split3(x):
    hi = x.astype(BF16).astype(F32)
    rest = x - hi
    mid = rest.astype(BF16).astype(F32)
    return hi, mid, rest - mid


def dot(a, b):
    return jnp.dot(a, b, preferred_element_type=F32)


def dot_nt(a, b):
    return lax.dot_general(a, b, (((1,), (1,)), ((), ())), preferred_element_type=F32)


def head_kernel(
    blocks_all,
    tiles,
    pos,
    vel,
    force,
    mass,
    feat,
    slots,
    w_feat,
    w_basis_t,
    bias,
    w_out,
    moved,
    payload,
    moved_v,
    half_v,
    mass_v,
    slots_v,
    w_basis_v,
    bias_v,
    w_out_v,
    count,
):
    atoms = pos.shape[2]
    here = atoms // TILE
    m = mass[...]
    parts = [[], [], []]
    for c in range(3):
        half = vel[c] + 0.5 * TIME_STEP * force[c] / m
        new = pos[c] + TIME_STEP * half
        moved[c] = new
        moved_v[c] = new
        half_v[c] = half
        for k, part in enumerate(split3(new)):
            parts[k].append(part)
    rows = parts[0] + parts[1] + parts[2] + [jnp.zeros((PAY - HID - 9, atoms), F32)]
    coords = jnp.concatenate(rows, axis=0).astype(BF16)
    projected = dot(w_feat[...], feat[0]).astype(BF16)
    local = slots[...] & (atoms - 1)
    atom_ids = lax.broadcasted_iota(I32, (atoms, atoms), 0)
    pick = jnp.where(atom_ids == local, 1.0, 0.0).astype(BF16)
    ordered = dot(jnp.concatenate([projected, coords], axis=0), pick).astype(BF16)
    for b in range(here):
        payload[b] = ordered[:, b * TILE : (b + 1) * TILE]
    mass_v[...] = m
    slots_v[...] = local
    w_basis_v[...] = w_basis_t[...]
    bias_v[...] = bias[...]
    w_out_v[...] = w_out[...]
    first = lax.axis_index("atom") * here
    for rb in range(here):
        for d in range(DELTAS):
            count[rb, d] = 0
        for j in range(DELTAS):
            off = tiles[rb, j] - (first + rb) + REACH
            off = jnp.where(off < 0, off + blocks_all, off)
            off = jnp.where(off >= blocks_all, off - blocks_all, off)
            count[rb, off] = count[rb, off] + 1


def lane_gather(table, index):
    rows = lax.GatherDimensionNumbers(
        offset_dims=(),
        collapsed_slice_dims=(1,),
        start_index_map=(1,),
        operand_batching_dims=(0,),
        start_indices_batching_dims=(0,),
    )
    return lax.gather(
        table,
        index[..., None],
        rows,
        slice_sizes=(1, 1),
        mode=lax.GatherScatterMode.PROMISE_IN_BOUNDS,
    )


def wrap(c, length):
    return c - length * jnp.floor(c * (1.0 / length) + 0.5)


def load_block(ref, b, at, flat_s, proj_s):
    block = ref[b].astype(F32)
    proj_s[at] = block[:HID]
    xyz = block[HID : HID + 3] + block[HID + 3 : HID + 6] + block[HID + 6 : HID + 9]
    plane = xyz[:2]
    plane = plane - SIDE_LENGTH * jnp.floor(plane * (1.0 / SIDE_LENGTH))
    flat_s[at] = jnp.concatenate([plane, xyz[2:], jnp.zeros((5, TILE), F32)], axis=0)


def visit_tiles(local, blocks_all, here, count_s, row_s, mine_s, lhs_s, base_s, wout_s, acc_s, scratch):
    (
        flat_s,
        proj_s,
        marks_s,
        list_s,
        index_s,
        geom_s,
        right_s,
        there_s,
        sum_s,
        rb_s,
        block_s,
        times_s,
        lift_s,
        pass_s,
        pass_rb_s,
        pass_block_s,
    ) = scratch
    first = lax.axis_index("atom") * here
    depth = blocks_all * LAYER_WIDTH
    lane = lax.broadcasted_iota(I32, (SUB, LANES), 1)
    group = lane // CAP

    found = jnp.int32(0)
    split = found
    for rb in range(here):
        if rb == 1:
            split = found
        for d in range(DELTAS):
            if (0 <= rb + d - REACH < here) != local:
                continue
            times = count_s[rb, d]
            source = first + rb + d - REACH
            rb_s[found] = rb
            block_s[found] = HALO * here + rb + d - REACH
            times_s[found] = times
            lift_s[found] = jnp.where(
                source < 0, depth, jnp.where(source >= blocks_all, -depth, 0.0)
            )
            found = found + jnp.where(times > 0, 1, 0)
    last = jnp.maximum(found - 1, 0)
    for k in range(BUILD):
        rb_s[found + k] = rb_s[last]
        block_s[found + k] = block_s[last]
        lift_s[found + k] = lift_s[last]
        times_s[found + k] = 0

    upper = (
        lax.broadcasted_iota(I32, (LANES, LANES), 0) <= lax.broadcasted_iota(I32, (LANES, LANES), 1)
    )
    upper = jnp.where(upper, 128.0, 0.0).astype(BF16)
    tag = (lax.broadcasted_iota(I32, (1, LANES), 1) * 129 + 16384 + 128).astype(F32)
    inside = CUTOFF * CUTOFF * 1.0001

    def build(k, q):
        rb, block = rb_s[q], block_s[q]
        d2 = None
        for c in range(3):
            there = flat_s[block, c : c + 1, :]
            if c == 2:
                diff = (there - lift_s[q]) - row_s[rb, c]
            else:
                diff = jnp.abs(there - row_s[rb, c])
                diff = jnp.minimum(diff, SIDE_LENGTH - diff)
            d2 = diff * diff if d2 is None else d2 + diff * diff
        near = d2 < inside
        mask = jnp.where(near, 1.0, 0.0)
        rank = dot(mask.astype(BF16), upper)
        fullest = jnp.max(rank).astype(I32)
        marks_s[k] = jnp.where(near, tag - rank, 0.0).astype(I32)
        passes = jnp.maximum((fullest + (128 * CAP - 1)) // (128 * CAP), 1)
        pass_s[q] = passes
        return passes

    def compact(k, q):
        v = marks_s[k].astype(jnp.int16)
        for bit in range(7):
            go = jnp.where((v & jnp.int16(128 << bit)) != jnp.int16(0), v, jnp.int16(0))
            v = (v ^ go) | pltpu.roll(go, LANES - (1 << bit), 1)
        v = v.astype(I32)
        for o in range(GROUPS):
            piece = v[SUB * o : SUB * (o + 1)]
            list_s[q, o] = piece if o == 0 else pltpu.roll(piece, CAP * o, 1)

    def build_some(i, totals):
        low, all_of = totals
        for k in range(BUILD):
            compact(k, jnp.where(i > 0, BUILD * (i - 1) + k, here * DELTAS + BUILD))
        for k in range(BUILD):
            q = jnp.minimum(BUILD * i + k, found)
            passes = jnp.where(q < found, build(k, q), 0)
            low = low + jnp.where(rb_s[q] == 0, passes, 0)
            all_of = all_of + passes
        return low, all_of

    for k in range(BUILD):
        marks_s[k] = jnp.zeros((TILE, LANES), I32)
    low, total = lax.fori_loop(0, (found + BUILD - 1) // BUILD + 1, build_some, (jnp.int32(0), jnp.int32(0)))
    odd = low & 1
    before = jnp.maximum(split - 1, 0)
    pass_s[before] = pass_s[before] + odd
    pairs = (total + odd + 1) // 2

    sharp = (BASIS_SHARPNESS * 1.4426950408889634) ** 0.5
    centre = (lax.broadcasted_iota(I32, (NB, 1), 0).astype(F32) + 0.5) * (CUTOFF / NB * sharp)

    def front(q, p, i, side):
        rb, block = rb_s[q], block_s[q]
        half = slice(LANES * side, LANES * (side + 1))
        pass_rb_s[i] = rb
        pass_block_s[i, side] = block
        times = jnp.where(p < GROUPS, times_s[q].astype(F32) * 2.0, 0.0)
        which = jnp.minimum(q, found - 1)
        here_group = (group - p) & (GROUPS - 1)
        level = [list_s[which, o] for o in range(GROUPS)]
        bit = 1
        while len(level) > 1:
            choose = (here_group & bit) != 0
            level = [
                jnp.where(choose, level[2 * k + 1], level[2 * k]) for k in range(len(level) // 2)
            ]
            bit *= 2
        slot = pltpu.roll(level[0], (LANES - CAP * p) & (LANES - 1), 1)
        idx = slot & (LANES - 1)
        index_s[i, :, half] = idx
        weight = jnp.where(slot >= 16384, times, 0.0)
        d2 = None
        for c in range(3):
            table = jnp.broadcast_to(flat_s[block, c : c + 1, :], (SUB, LANES))
            there = jnp.take_along_axis(table, idx, axis=1, mode="promise_in_bounds")
            one = there - mine_s[rb, c]
            one = one - lift_s[q] if c == 2 else wrap(one, SIDE_LENGTH)
            geom_s[i, c, :, half] = one
            d2 = one * one if d2 is None else d2 + one * one
        distance = jnp.sqrt(d2 + SOFTEN)
        inner_part = jnp.maximum(1.0 - d2 * (1.0 / (CUTOFF * CUTOFF)), 0.0)
        weight = weight * inner_part
        geom_s[i, 3, :, half] = distance * sharp
        geom_s[i, 4, :, half] = weight * inner_part * ((-BASIS_SHARPNESS / sharp) / distance)
        geom_s[i, 5, :, half] = weight * (-2.0 / (CUTOFF * CUTOFF))

    def advance(q, p):
        last = p + 1 >= pass_s[q]
        return jnp.where(last, q + 1, q), jnp.where(last, 0, p + 1)

    pass_s[found] = 1 << 20

    def front_some(i, state):
        q, p = state
        for k in range(2 * UNROLL):
            front(q, p, i * UNROLL + k // 2, k % 2)
            q, p = advance(q, p)
        return q, p

    turns = (pairs + (UNROLL - 1)) // UNROLL
    lax.fori_loop(0, turns, front_some, (jnp.int32(0), jnp.int32(0)))

    def first_half(i, u, r):
        offset = geom_s[i, 3, r : r + 1, :] - centre
        basis = jnp.exp2(-(offset * offset))
        right_s[u, r, 0:NB] = basis.astype(BF16)
        right_s[u, r, NB : 2 * NB] = (offset * basis).astype(BF16)
        base = base_s[pass_rb_s[i], r]
        for side in range(2):
            half = slice(LANES * side, LANES * (side + 1))
            at = jnp.broadcast_to(index_s[i, r : r + 1, half], (HID, LANES))
            there_s[u, r, :, half] = lane_gather(proj_s[pass_block_s[i, side]], at) + base

    def fold(x):
        part = x[0:SUB]
        for k in range(1, x.shape[0] // SUB):
            part = part + x[SUB * k : SUB * (k + 1)]
        return part

    def second_half(u, r):
        both = dot(lhs_s[...], right_s[u, r])
        act = jnp.tanh(both[:HID] + there_s[u, r])
        w_o = wout_s[...]
        w_o = jnp.concatenate([w_o, w_o], axis=1)
        share = w_o * act
        energy = fold(share)
        grad = fold((w_o - share * act) * both[HID:])
        for side in range(2):
            half = slice(LANES * side, LANES * (side + 1))
            sum_s[u, side, SUB * r : SUB * (r + 1)] = energy[:, half]
            sum_s[u, 2 + side, SUB * r : SUB * (r + 1)] = grad[:, half]

    def last_part(i, u):
        sums = []
        for k in range(4):
            one = sum_s[u, k, pl.ds(0, SUB, stride=SUB)]
            for j in range(1, SUB):
                one = one + sum_s[u, k, pl.ds(j, SUB, stride=SUB)]
            sums.append(one)
        energy = jnp.concatenate(sums[:2], axis=1)
        grad = jnp.concatenate(sums[2:], axis=1)
        coef = geom_s[i, 5] * energy + geom_s[i, 4] * grad
        rb = pass_rb_s[i]
        for c in range(3):
            acc_s[rb, c] = acc_s[rb, c] + coef * geom_s[i, c]

    def step(i, carry):
        for u in range(UNROLL):
            for r in range(SUB):
                first_half(UNROLL * i + u, u, r)
                second_half(u, r)
        for u in range(UNROLL):
            last_part(UNROLL * i + u, u)
        return carry

    lax.fori_loop(0, turns, step, 0)


def local_kernel(
    blocks_all, count, w_basis_t, bias, w_out, own, acc_s, row_s, mine_s, lhs_s, base_s, wout_s, *scratch
):
    here = own.shape[0]
    flat_s, proj_s = scratch[:2]
    lane = lax.broadcasted_iota(I32, (SUB, LANES), 1)
    group = lane // CAP
    for b in range(here):
        load_block(own, b, HALO * here + b, flat_s, proj_s)

    w_basis = jnp.transpose(w_basis_t[...].astype(F32)).astype(BF16)
    eye = lax.broadcasted_iota(I32, (HID, HID), 0) == lax.broadcasted_iota(I32, (HID, HID), 1)
    bias_col = jnp.sum(jnp.where(eye, bias[...], 0.0), axis=1, keepdims=True)
    wout_col = jnp.sum(jnp.where(eye, w_out[...], 0.0), axis=1, keepdims=True)
    wout_s[...] = jnp.broadcast_to(wout_col, (HID, LANES))

    wide_r = lax.broadcasted_iota(I32, (NB, 2 * NB), 0)
    wide_c = lax.broadcasted_iota(I32, (NB, 2 * NB), 1)
    for k in range(2):
        spread = jnp.where(wide_r + NB * k == wide_c, 1.0, 0.0).astype(BF16)
        lhs_s[HID * k : HID * (k + 1)] = dot(w_basis, spread).astype(BF16)

    row_l = lax.broadcasted_iota(I32, (TILE, LANES), 0)
    row_of = (lax.broadcasted_iota(I32, (TILE, LANES), 1) // CAP) * SUB
    for r in range(SUB):
        sel = jnp.where(row_l == row_of + r, 1.0, 0.0).astype(BF16)
        for rb in range(here):
            base_s[rb, r] = dot(own[rb, :HID, :], sel) + bias_col

    for rb in range(here):
        own_block = HALO * here + rb
        cols = jnp.transpose(flat_s[own_block])
        for c in range(3):
            row_s[rb, c] = jnp.broadcast_to(cols[:, c : c + 1], (TILE, LANES))
        for c in range(3):
            m = jnp.zeros((SUB, LANES), F32)
            for o in range(GROUPS):
                m = jnp.where(group == o, row_s[rb, c, SUB * o : SUB * (o + 1)], m)
            mine_s[rb, c] = m
            acc_s[rb, c] = jnp.zeros((SUB, 2 * LANES), F32)

    visit_tiles(True, blocks_all, here, count, row_s, mine_s, lhs_s, base_s, wout_s, acc_s, scratch)


def far_kernel(
    blocks_all,
    count,
    half,
    mass,
    slots,
    one_a,
    one_b,
    two_a,
    two_b,
    moved,
    bead_one,
    bead_two,
    acc_local,
    row_s,
    mine_s,
    lhs_s,
    base_s,
    wout_s,
    vel_next,
    force_next,
    acc_s,
    *scratch,
):
    atoms = half.shape[2]
    here = atoms // TILE
    flat_s, proj_s = scratch[:2]
    lane = lax.broadcasted_iota(I32, (SUB, LANES), 1)
    sub = lax.broadcasted_iota(I32, (SUB, LANES), 0)
    acc_s[...] = acc_local[...]
    place = lax.axis_index("atom")
    side_one = jnp.where((place & 1) == 0, 1, -1)
    side_two = jnp.where((place & 2) == 0, 2, -2)
    sources = ((one_a, side_one), (one_b, -side_one), (two_a, side_two), (two_b, -side_two))
    for ref, away in sources:
        for b in range(here):
            at = (HALO + away) * here + b
            load_block(ref, b, at, flat_s, proj_s)

    visit_tiles(False, blocks_all, here, count, row_s, mine_s, lhs_s, base_s, wout_s, acc_s, scratch)

    forces = []
    for rb in range(here):
        rows = []
        for c in range(3):
            a = acc_s[rb, c, :, :LANES] + acc_s[rb, c, :, LANES:]
            for step in (1, 2, 4):
                down = pltpu.roll(a, LANES - step, 1)
                up = pltpu.roll(a, step, 1)
                a = a + jnp.where((lane & step) == 0, down, up)
            a = jnp.where((lane & (CAP - 1)) == sub, a, 0.0)
            rows.append(jnp.sum(a, axis=0, keepdims=True))
        forces.append(rows)

    full = [jnp.concatenate([forces[rb][c] for rb in range(here)], axis=1) for c in range(3)]
    parts = [split3(f) for f in full]
    stacked = [parts[c][k] for k in range(3) for c in range(3)]
    stacked = jnp.concatenate(stacked + [jnp.zeros((7, atoms), F32)], axis=0).astype(BF16)
    atom_ids = lax.broadcasted_iota(I32, (atoms, atoms), 0)
    pick = jnp.where(atom_ids == slots[...], 1.0, 0.0).astype(BF16)
    placed = dot_nt(stacked, pick)
    m = mass[...]
    for c in range(3):
        pair = placed[c : c + 1] + placed[3 + c : 4 + c] + placed[6 + c : 7 + c]
        spring = -OMEGA_SQ * m * (2.0 * moved[c] - bead_one[c] - bead_two[c])
        total_force = pair + spring
        force_next[c] = total_force
        vel_next[c] = half[c] + 0.5 * TIME_STEP * total_force / m


def in_vmem(x):
    return pltpu.with_memory_space_constraint(x, pltpu.VMEM)


def in_smem(x):
    return pltpu.with_memory_space_constraint(x, pltpu.SMEM)


def swapped(block, axis, step, other):
    count = lax.axis_size(axis)
    route = []
    for i in range(count):
        up = ((i // step) % 2 == 0) != other
        route.append((i, (i + step if up else i - step) % count))
    return lax.ppermute(block, axis, route)


def body(
    positions,
    velocities,
    forces_now,
    masses,
    features,
    tile_blocks,
    block_slots,
    w_basis,
    w_feat,
    hidden_bias,
    w_out,
):
    atoms = positions.shape[2]
    here = atoms // TILE
    blocks_all = here * lax.axis_size("atom")
    mass = masses.reshape(1, atoms)
    slots = block_slots.reshape(1, atoms)
    vmem = pl.BlockSpec(memory_space=pltpu.VMEM)
    smem = pl.BlockSpec(memory_space=pltpu.SMEM)
    moved, payload, moved_v, half, mass_v, slots_v, w_basis_v, bias_v, w_out_v, count = pl.pallas_call(
        functools.partial(head_kernel, blocks_all),
        out_shape=(
            jax.ShapeDtypeStruct(positions.shape, F32),
            pltpu.VMEM((here, PAY, TILE), BF16),
            pltpu.VMEM(positions.shape, F32),
            pltpu.VMEM(positions.shape, F32),
            pltpu.VMEM((1, atoms), F32),
            pltpu.VMEM((1, atoms), I32),
            pltpu.VMEM((NB, HID), BF16),
            pltpu.VMEM((1, HID), F32),
            pltpu.VMEM((1, HID), F32),
            pltpu.SMEM((here, DELTAS), I32),
        ),
        in_specs=[smem] + [vmem] * 10,
        out_specs=(vmem,) * 9 + (smem,),
        name="head",
    )(
        tile_blocks,
        positions,
        velocities,
        forces_now,
        mass,
        features,
        slots,
        w_feat,
        w_basis.T,
        hidden_bias.reshape(1, HID),
        w_out.reshape(1, HID),
    )

    bead_one = swapped(moved_v, "bead", 1, False)
    bead_two = swapped(moved_v, "bead", 1, True)
    near = [
        swapped(payload, "atom", 1, False),
        swapped(payload, "atom", 1, True),
        swapped(payload, "atom", 2, False),
        swapped(payload, "atom", 2, True),
    ]
    sources = 2 * HALO + 1

    tile_room = here * DELTAS
    room = tile_room * GROUPS // 2 + 16
    scratch = [
        pltpu.VMEM((sources * here, SUB, TILE), F32),
        pltpu.VMEM((sources * here, HID, TILE), F32),
        pltpu.VMEM((BUILD, TILE, LANES), I32),
        pltpu.VMEM((tile_room + BUILD + 1, GROUPS, SUB, LANES), I32),
        pltpu.VMEM((room, SUB, 2 * LANES), I32),
        pltpu.VMEM((room, 6, SUB, 2 * LANES), F32),
        pltpu.VMEM((UNROLL, SUB, 2 * NB, 2 * LANES), BF16),
        pltpu.VMEM((UNROLL, SUB, HID, 2 * LANES), F32),
        pltpu.VMEM((UNROLL, 4, SUB * SUB, LANES), F32),
        pltpu.SMEM((tile_room + BUILD,), I32),
        pltpu.SMEM((tile_room + BUILD,), I32),
        pltpu.SMEM((tile_room + BUILD,), I32),
        pltpu.SMEM((tile_room + BUILD,), F32),
        pltpu.SMEM((tile_room + BUILD,), I32),
        pltpu.SMEM((room,), I32),
        pltpu.SMEM((room, 2), I32),
    ]

    acc_shape = (here, 3, SUB, 2 * LANES)
    tables = pl.pallas_call(
        functools.partial(local_kernel, blocks_all),
        out_shape=(
            pltpu.VMEM(acc_shape, F32),
            pltpu.VMEM((here, 3, TILE, LANES), F32),
            pltpu.VMEM((here, 3, SUB, LANES), F32),
            pltpu.VMEM((2 * HID, 2 * NB), BF16),
            pltpu.VMEM((here, SUB, HID, LANES), F32),
            pltpu.VMEM((HID, LANES), F32),
        ),
        in_specs=[smem] + [vmem] * 4,
        out_specs=(vmem,) * 6,
        scratch_shapes=scratch,
        cost_estimate=pl.CostEstimate(flops=3_000_000_000, bytes_accessed=2_000_000, transcendentals=0),
        name="near",
    )(in_smem(count), *(in_vmem(x) for x in (w_basis_v, bias_v, w_out_v, payload)))
    vel_next, force_next = pl.pallas_call(
        functools.partial(far_kernel, blocks_all),
        out_shape=(
            jax.ShapeDtypeStruct(positions.shape, F32),
            jax.ShapeDtypeStruct(positions.shape, F32),
        ),
        in_specs=[smem] + [vmem] * 16,
        out_specs=(vmem, vmem),
        scratch_shapes=[pltpu.VMEM(acc_shape, F32)] + scratch,
        name="far",
    )(
        in_smem(count),
        *(in_vmem(x) for x in (half, mass_v, slots_v, *near)),
        *(in_vmem(x) for x in (moved_v, bead_one, bead_two, *tables)),
    )
    return (moved, vel_next, force_next)


def solution(mesh):
    return jax.shard_map(
        body,
        mesh=mesh,
        in_specs=(
            P(None, "bead", "atom"),
            P(None, "bead", "atom"),
            P(None, "bead", "atom"),
            P("atom"),
            P("bead", None, "atom"),
            P("atom", None),
            P("atom"),
            P(),
            P(),
            P(),
            P(),
        ),
        out_specs=(P(None, "bead", "atom"), P(None, "bead", "atom"), P(None, "bead", "atom")),
        check_vma=False,
    )
```
